32 devices in a mesh: groups: 2 (over y), outer: 4 (over x, core), inner: 4 (over z).
Axes of the slice: x: 2, y: 2, z: 4, core: 2. Of those that a mesh axis runs over, the one named last changes fastest.
Arguments:
- activations: bfloat16 [4096, 8192], P(('groups', 'outer', 'inner')), parts along dimension 0, may hold values from -64 to 64
- upstream: bfloat16 [4096, 768], P(('groups', 'outer', 'inner')), parts along dimension 0, may hold values from -8 to 8
- frozen_weight_matrix: bfloat16 [8192, 768], P(('outer', 'inner')), may hold values from -0.21875 to 0.21875
- master: float32 [1146880], P(('groups', 'outer', 'inner')), parts along dimension 0, may hold values from -6 to 6
- moment: float32 [1146880], P(('groups', 'outer', 'inner')), parts along dimension 0, may hold values from -3 to 3
- second_moment: float32 [1146880], P(('groups', 'outer', 'inner')), parts along dimension 0, may hold values from 0.01 to 1
Outputs:
- input_gradient_rows: bfloat16 [4096, 8192], P(('groups', 'outer', 'inner')), parts along dimension 0
- new_master: float32 [1146880], P(('groups', 'outer', 'inner')), parts along dimension 0
- new_moment: float32 [1146880], P(('groups', 'outer', 'inner')), parts along dimension 0
- new_second: float32 [1146880], P(('groups', 'outer', 'inner')), parts along dimension 0
The draws below stay inside these ranges and needn't reach their ends.
There are 2 independent parts, one for each index of `groups`. The reference program is written for one: setup_inputs(seed, part) draws one part's arguments, and reference() takes and returns one part's arrays. A program takes and returns all parts, laid end to end along the dimension named above; an argument that names none is the same for every part. Nothing has to cross between parts.
All inputs are finite; a program needn't handle non-finite values.
Results may differ from the reference program's by a relative error of at most 0.001.
The reference program's roundings to bfloat16 on the way count: a program that leaves them out, or rounds other values in their place, can miss the bound.
Values may be sent and summed in bfloat16 or wider, within the bound.
No kernel may reach another device: no remote copies, remote signals or barrier semaphores. Data moves between devices by JAX's collectives and lax.ppermute only.
A program may use at most 128 MiB of HBM per device.

```python
import math
import jax
import jax.numpy as jnp

D = 8192
VALUE_CHANNELS = 768
ADAPTER_RANK = 64
TOKENS = 2048
PARAMS = 573440


def draw_activations(key, part):
    keys = jax.random.split(jax.random.fold_in(key, 11), 5)
    column_scale = jnp.exp(jnp.log(10.0) * jax.random.uniform(keys[1], (D,), jnp.float32))
    row_scale = jnp.exp(jnp.log(10.0) * jax.random.uniform(keys[2], (TOKENS, 1), jnp.float32))
    offset = jax.random.normal(keys[4], (D,), jnp.float32)
    values = jax.random.normal(keys[0], (TOKENS, D), jnp.float32) + 0.2 * offset
    return jnp.clip(0.1 * values * row_scale * column_scale, -64.0, 64.0).astype(jnp.bfloat16)


def draw_upstream(key, part):
    keys = jax.random.split(jax.random.fold_in(key, 23), 2)
    offset = jax.random.normal(keys[1], (VALUE_CHANNELS,), jnp.float32)
    values = jax.random.normal(keys[0], (TOKENS, VALUE_CHANNELS), jnp.float32) + 0.2 * offset
    return jnp.clip(values, -8.0, 8.0).astype(jnp.bfloat16)


def block_scale(rng, shape, shards, smallest, high):
    def one(axis_at, parts):
        draws = jax.random.uniform(jax.random.fold_in(jax.random.fold_in(rng, 6), axis_at), (parts,), jnp.float32, smallest / len(shards), high / len(shards))
        return jnp.repeat(jnp.exp(draws), shape[axis_at] // parts).reshape((-1,) + (1,) * (len(shape) - axis_at - 1))

    factor_of = one(*shards[0])
    for cut in shards[1:]:
        factor_of = factor_of * one(*cut)
    return factor_of


def gaussian(stream_key, dims, width, most, cuts=(), dtype=jnp.bfloat16):
    result = jax.random.normal(stream_key, dims, jnp.float32) * width
    if len(cuts) > 0:
        result = block_scale(stream_key, dims, cuts, -0.22, 0.18) * result
    return jnp.clip(result, min=-most, max=most).astype(dtype)


def setup_inputs(seed: int = 0, part: int = 0) -> dict:
    seeds = jax.random.split(jax.random.key(seed), 7)
    part_splits = jax.random.split(jax.random.fold_in(seeds[6], part), 7)
    activations = draw_activations(jax.random.fold_in(jax.random.fold_in(seeds[6], part), 71), part)
    upstream = draw_upstream(jax.random.fold_in(jax.random.fold_in(seeds[6], part), 71), part)
    frozen_weight_matrix = gaussian(seeds[2], (D, VALUE_CHANNELS), VALUE_CHANNELS ** -0.5, 0.21875, ((0, 16),))
    master = gaussian(part_splits[3], (PARAMS,), 1.0, 6.0, ((0, 16),), jnp.float32)
    moment = gaussian(part_splits[4], (PARAMS,), 0.3, 3.0, ((0, 16),), jnp.float32)
    second_moment = jnp.clip(jnp.exp(math.log(1.0) - 4.6051702 * jax.random.uniform(part_splits[5], (PARAMS,), jnp.float32) ** block_scale(part_splits[5], (PARAMS,), ((0, 16),), -0.2, 0.2)), 0.01, 1.0)
    return dict(activations=activations, upstream=upstream, frozen_weight_matrix=frozen_weight_matrix, master=master, moment=moment, second_moment=second_moment)


def reference(activations, upstream, frozen_weight_matrix, master, moment, second_moment):
    adapter_scale_factor = 0.5 / math.sqrt(ADAPTER_RANK * VALUE_CHANNELS)
    working = master.astype(jnp.bfloat16)
    down_weight_transposed = working[:ADAPTER_RANK * D].reshape(ADAPTER_RANK, D)
    up_m = working[ADAPTER_RANK * D:].reshape(ADAPTER_RANK, VALUE_CHANNELS)
    rank_gradient = jnp.dot(upstream, up_m.T, preferred_element_type=jnp.float32).astype(jnp.bfloat16)
    input_gradient_rows = (jnp.dot(upstream, frozen_weight_matrix.T, preferred_element_type=jnp.float32) + adapter_scale_factor * jnp.dot(rank_gradient, down_weight_transposed, preferred_element_type=jnp.float32)).astype(jnp.bfloat16)
    projected_rows = jnp.dot(activations, down_weight_transposed.T, preferred_element_type=jnp.float32).astype(jnp.bfloat16)
    down_weight_gradient = adapter_scale_factor * jnp.dot(rank_gradient.T, activations, preferred_element_type=jnp.float32)
    up_weight_gradient = adapter_scale_factor * jnp.dot(projected_rows.T, upstream, preferred_element_type=jnp.float32)
    flat_grad = jnp.concatenate([down_weight_gradient.reshape(-1), up_weight_gradient.reshape(-1)])
    norm = jnp.sqrt(jnp.sum(flat_grad * flat_grad) + 1e-06)
    clipped = flat_grad * jnp.minimum(1.0, math.sqrt(PARAMS) / norm)
    new_moment = 0.9 * moment + 0.1 * clipped
    new_second = 0.999 * second_moment + 0.001 * clipped * clipped
    corr_one = 1.0 - 0.9 ** 10
    corr_two = 1.0 - 0.999 ** 10
    new_master = master - 0.1 * (new_moment / corr_one) / (jnp.sqrt(new_second / corr_two) + 1e-08)
    return (input_gradient_rows, new_master, new_moment, new_second)
```

```python
import functools
import math

import jax
import jax.numpy as jnp
from jax import lax
from jax.experimental import pallas as pl
from jax.experimental.pallas import tpu as pltpu
from jax.sharding import PartitionSpec as P

LANES = 128


def per_device_general(activations, upstream, frozen_weight_matrix, master, moment, second_moment):
    width = activations.shape[1]
    value_width = upstream.shape[1]
    whole = lax.all_gather(master.astype(jnp.bfloat16), ("outer", "inner"), axis=0, tiled=True)
    rank_activations = whole.shape[0] // (width + value_width)
    adapter_scale_factor = 0.5 / math.sqrt(rank_activations * value_width)
    down_weight_transposed = whole[: rank_activations * width].reshape(rank_activations, width)
    up_m = whole[rank_activations * width :].reshape(rank_activations, value_width)
    rank_gradient = jnp.dot(upstream, up_m.T, preferred_element_type=jnp.float32).astype(
        jnp.bfloat16
    )
    projected_rows = jnp.dot(
        activations, down_weight_transposed.T, preferred_element_type=jnp.float32
    ).astype(jnp.bfloat16)
    down_weight_gradient = adapter_scale_factor * jnp.dot(
        rank_gradient.T, activations, preferred_element_type=jnp.float32
    )
    up_weight_gradient = adapter_scale_factor * jnp.dot(
        projected_rows.T, upstream, preferred_element_type=jnp.float32
    )
    flat_grad = jnp.concatenate([down_weight_gradient.reshape(-1), up_weight_gradient.reshape(-1)])
    grad_shard = lax.psum_scatter(flat_grad, ("outer", "inner"), scatter_dimension=0, tiled=True)
    sum_squares = lax.psum(jnp.sum(grad_shard * grad_shard), ("outer", "inner"))
    feat_rows = frozen_weight_matrix.shape[0]
    feat_start = lax.axis_index(("outer", "inner")) * feat_rows
    own_cols = lax.dynamic_slice_in_dim(down_weight_transposed, feat_start, feat_rows, 1)
    tok_piece = lax.all_gather(upstream, ("outer", "inner"), axis=0, tiled=True)
    rank_piece = jnp.dot(tok_piece, up_m.T, preferred_element_type=jnp.float32).astype(jnp.bfloat16)
    frozen_output = lax.dot_general(
        tok_piece,
        frozen_weight_matrix,
        (((1,), (1,)), ((), ())),
        preferred_element_type=jnp.float32,
    )
    feat_block = (
        frozen_output
        + adapter_scale_factor * jnp.dot(rank_piece, own_cols, preferred_element_type=jnp.float32)
    ).astype(jnp.bfloat16)
    n_outer = lax.axis_size("outer")
    n_inner = lax.axis_size("inner")
    tok_count = upstream.shape[0]
    reordered = (
        feat_block.reshape(n_outer, n_inner, tok_count, feat_rows)
        .transpose(1, 0, 2, 3)
        .reshape(n_inner * n_outer * tok_count, feat_rows)
    )
    input_gradient_rows = lax.all_to_all(
        lax.all_to_all(reordered, "inner", split_axis=0, concat_axis=1, tiled=True),
        "outer",
        split_axis=0,
        concat_axis=1,
        tiled=True,
    )
    return (input_gradient_rows,) + adam(
        grad_shard, sum_squares, whole.shape[0], master, moment, second_moment
    )


def adam(grad_shard, sum_squares, params, master, moment, second_moment):
    norm = jnp.sqrt(sum_squares + 1e-06)
    clipped = grad_shard * jnp.minimum(1.0, math.sqrt(params) / norm)
    new_moment = 0.9 * moment + 0.1 * clipped
    new_second = 0.999 * second_moment + 0.001 * clipped * clipped
    corr_one = 1.0 - 0.9**10
    corr_two = 1.0 - 0.999**10
    new_master = master - 0.1 * (new_moment / corr_one) / (jnp.sqrt(new_second / corr_two) + 1e-08)
    return new_master, new_moment, new_second


def dot_t(a, b):
    return lax.dot_general(a, b, (((1,), (1,)), ((), ())), preferred_element_type=jnp.float32)


def t_dot(a, b):
    return lax.dot_general(a, b, (((0,), (0,)), ((), ())), preferred_element_type=jnp.float32)


def grads_kernel(
    rank, scale, where_ref, act_ref, ups_ref, own_ref, z1_ref, z2_ref, z3_ref,
    x_ref, c_ref, cx_ref, keep_ref, send_ref, up_ref, cols_ref, flat, down,
):
    o, z = where_ref[0], where_ref[1]
    rows = own_ref.shape[0]
    width = act_ref.shape[1]
    value_width = ups_ref.shape[1]
    n_in = 4

    def place(outer, back, block):
        at = (outer * n_in + lax.rem(z + n_in - back, n_in)) * rows
        flat[pl.ds(pl.multiple_of(at, 8), rows), :] = block.astype(jnp.float32)

    for back, ref in enumerate((own_ref, z1_ref, z2_ref, z3_ref)):
        place(o, back, ref[...])
    x = o // 2
    c = lax.rem(o, 2)
    ox, oc, ocx = (1 - x) * 2 + c, x * 2 + 1 - c, (1 - x) * 2 + 1 - c
    for back in range(n_in):
        place(ox, back, x_ref[back])
        place(oc, back, c_ref[back])
        place(ocx, back, cx_ref[back])

    tiles = width // LANES
    for j in range(tiles):
        down[:, j * LANES : (j + 1) * LANES] = flat[pl.ds(j, rank, stride=tiles), :].astype(
            jnp.bfloat16
        )
    up_tiles = value_width // LANES
    base = rank * tiles
    for j in range(up_tiles):
        up_ref[:, j * LANES : (j + 1) * LANES] = flat[
            pl.ds(base + j, rank, stride=up_tiles), :
        ].astype(jnp.bfloat16)

    share = cols_ref.shape[1]
    cols_ref[...] = down[:, pl.ds(pl.multiple_of(o * share, LANES), share)]

    ups = ups_ref[...]
    back_rank = dot_t(ups, up_ref[...]).astype(jnp.bfloat16)
    projected = dot_t(act_ref[...], down[...]).astype(jnp.bfloat16)
    grad_up = scale * t_dot(projected, ups)
    for j in range(up_tiles):
        flat[pl.ds(base + j, rank, stride=up_tiles), :] = grad_up[:, j * LANES : (j + 1) * LANES]
    step = 8
    for j0 in range(0, tiles, step):
        part = scale * t_dot(back_rank, act_ref[:, j0 * LANES : (j0 + step) * LANES])
        for j in range(step):
            flat[pl.ds(j0 + j, rank, stride=tiles), :] = part[:, j * LANES : (j + 1) * LANES]

    for core, ref in ((c, keep_ref), (1 - c, send_ref)):
        for k, xx in enumerate((1 - x, x)):
            for ahead in range(n_in):
                at = ((xx * 2 + core) * n_in + lax.rem(z + ahead, n_in)) * rows
                ref[k, ahead] = flat[pl.ds(pl.multiple_of(at, 8), rows), :]


def outs_kernel(scale, halves, where_ref, *refs):
    u_refs, w_refs = refs[:4], refs[4 : 4 + halves]
    up_ref, cols_ref, own_ref, core_ref, x_ref = refs[4 + halves :]
    y, z, back = where_ref[2], where_ref[1], where_ref[3]
    feats = own_ref.shape[1]
    at = lax.rem(z + 4 - back, 4) * feats
    up = up_ref[...]
    outs = (own_ref, core_ref, x_ref.at[0], x_ref.at[1])
    ranks = [dot_t(u[...], up).astype(jnp.bfloat16) for u in u_refs]
    for h, w_ref in enumerate(w_refs):
        n = w_ref.shape[0]
        first = 0 if halves == 1 else (y if h == 0 else 1 - y) * n
        cols = cols_ref[:, pl.ds(pl.multiple_of(at + first, LANES), n)]
        w = w_ref[...]
        for u, r, out in zip(u_refs, ranks, outs):
            low = jnp.dot(r, cols, preferred_element_type=jnp.float32)
            value = (dot_t(u[...], w) + scale * low).astype(jnp.bfloat16)
            if halves == 1:
                out[...] = value
            else:
                out[:, pl.ds(pl.multiple_of(first, LANES), n)] = value


def assemble_kernel(n, where_ref, *refs):
    blocks, (out_ref, sem) = refs[:-2], refs[-2:]
    o, z = where_ref[0], where_ref[1]
    x, c = o // 2, lax.rem(o, 2)
    outers = (o, x * 2 + 1 - c, (1 - x) * 2 + c, (1 - x) * 2 + 1 - c)
    copies = []
    k = 0
    for back in range(n):
        zz = lax.rem(z + n - back, n)
        for src in range(4):
            ref = blocks[back * 4 + src]
            if len(ref.shape) == 3:
                ref = ref.at[0]
            feats = ref.shape[1]
            at = (outers[src] * n + zz) * feats
            dst = out_ref.at[:, pl.ds(pl.multiple_of(at, LANES), feats)]
            copies.append(pltpu.make_async_copy(ref, dst, sem.at[k]))
            copies[-1].start()
            k += 1
    for copy in copies:
        copy.wait()


def vmem(n):
    return [pl.BlockSpec(memory_space=pltpu.VMEM)] * n


SMEM = pl.BlockSpec(memory_space=pltpu.SMEM)


def shift(value, s, n):
    return lax.ppermute(value, "inner", [(i, (i + s) % n) for i in range(n)])


def swap(value, bit, n):
    return lax.ppermute(value, "outer", [(i, i ^ bit) for i in range(n)])


def per_device_permutes(rank, activations, upstream, frozen_weight_matrix, master, moment, second_moment):
    n_out, n_in = 4, 4
    tokens, width = activations.shape
    value_width = upstream.shape[1]
    feats = frozen_weight_matrix.shape[0]
    rows = master.shape[0] // LANES
    scale = 0.5 / math.sqrt(rank * value_width)
    y, o, z = lax.axis_index("groups"), lax.axis_index("outer"), lax.axis_index("inner")
    bf16, f32 = jnp.bfloat16, jnp.float32

    def where(back=0):
        return jnp.stack([o, z, y, jnp.int32(back)]).astype(jnp.int32)

    p = master.astype(bf16).reshape(rows, LANES)
    pz = [shift(p, s, n_in) for s in range(1, n_in)]
    zb = jnp.stack([p] + pz)
    xb = swap(zb, 2, n_out)
    cb = swap(zb, 1, n_out)
    cxb = swap(xb, 1, n_out)

    uc = swap(upstream, 1, n_out)
    ux = swap(upstream, 2, n_out)
    ucx = swap(ux, 1, n_out)

    half = lax.dynamic_slice_in_dim(frozen_weight_matrix, y * (feats // 2), feats // 2, 0)
    wz = [shift(half, s, n_in) for s in range(1, n_in)]
    wy = [lax.ppermute(w, "groups", [(0, 1), (1, 0)]) for w in wz]

    blocks = jax.ShapeDtypeStruct((2, n_in, rows, LANES), f32)
    keep, send, up_m, cols = pl.pallas_call(
        functools.partial(grads_kernel, rank, scale),
        out_shape=(
            blocks,
            blocks,
            jax.ShapeDtypeStruct((rank, value_width), bf16),
            jax.ShapeDtypeStruct((rank, n_in * feats), bf16),
        ),
        in_specs=[SMEM] + vmem(9),
        out_specs=tuple(vmem(4)),
        scratch_shapes=[
            pltpu.VMEM((n_out * n_in * rows, LANES), f32),
            pltpu.VMEM((rank, width), bf16),
        ],
        name="local_grads",
    )(where(), activations, upstream, p, *pz, xb, cb, cxb)

    rc = swap(send, 1, n_out)
    rx = swap(keep[0] + rc[0], 2, n_out)
    mine = keep[1] + rc[1] + rx
    rz = [shift(mine[s], s, n_in) for s in range(1, n_in)]
    grad = mine[0] + rz[0] + rz[1] + rz[2]
    squares = jnp.sum((grad * grad).reshape(rows // 8, 8, LANES), axis=0)
    squares = squares + swap(squares, 1, n_out)
    squares = squares + swap(squares, 2, n_out)
    sz = [shift(squares, s, n_in) for s in range(1, n_in)]
    sum_squares = jnp.sum(squares + sz[0] + sz[1] + sz[2])

    pieces = []
    for back in range(n_in):
        ws = [frozen_weight_matrix] if back == 0 else [wz[back - 1], wy[back - 1]]
        piece = jax.ShapeDtypeStruct((tokens, feats), bf16)
        own, core, far = pl.pallas_call(
            functools.partial(outs_kernel, scale, len(ws)),
            out_shape=(piece, piece, jax.ShapeDtypeStruct((2, tokens, feats), bf16)),
            in_specs=[SMEM] + vmem(4 + len(ws) + 2),
            out_specs=tuple(vmem(3)),
            name="outs",
        )(where(back), upstream, uc, ux, ucx, *ws, up_m, cols)
        from_core = swap(core, 1, n_out)
        from_x = swap(far, 2, n_out)
        from_cx = swap(from_x[1], 1, n_out)
        pieces += [own, from_core, from_x, from_cx]
    input_gradient_rows = pl.pallas_call(
        functools.partial(assemble_kernel, n_in),
        out_shape=jax.ShapeDtypeStruct((tokens, width), bf16),
        in_specs=[SMEM] + [pl.BlockSpec(memory_space=pltpu.VMEM)] * 16,
        out_specs=pl.BlockSpec(memory_space=pl.ANY),
        scratch_shapes=[pltpu.SemaphoreType.DMA((16,))],
        name="assemble",
    )(where(), *pieces)
    return (input_gradient_rows,) + adam(
        grad.reshape(-1), sum_squares, n_out * n_in * master.shape[0], master, moment, second_moment
    )


def solution(mesh):
    sizes = (mesh.shape["groups"], mesh.shape["outer"], mesh.shape["inner"])

    def per_device(activations, upstream, frozen_weight_matrix, master, moment, second_moment):
        n = sizes[1] * sizes[2]
        width, value_width = activations.shape[1], upstream.shape[1]
        rank = n * master.shape[0] // (width + value_width)
        args = (activations, upstream, frozen_weight_matrix, master, moment, second_moment)
        if sizes == (2, 4, 4) and master.shape[0] % (8 * LANES) == 0:
            return per_device_permutes(rank, *args)
        return per_device_general(*args)

    return jax.shard_map(
        per_device,
        mesh=mesh,
        in_specs=(
            P(("groups", "outer", "inner"), None),
            P(("groups", "outer", "inner"), None),
            P(("outer", "inner"), None),
            P(("groups", "outer", "inner")),
            P(("groups", "outer", "inner")),
            P(("groups", "outer", "inner")),
        ),
        out_specs=(
            P(("groups", "outer", "inner"), None),
            P(("groups", "outer", "inner")),
            P(("groups", "outer", "inner")),
            P(("groups", "outer", "inner")),
        ),
        check_vma=False,
    )
```
